32 devices in a mesh: row: 4 (over x, core), col: 8 (over z, y).
Axes of the slice: x: 2, y: 2, z: 4, core: 2. Of those that a mesh axis runs over, the one named last changes fastest.
Arguments:
- vectors: float32 [8, 4096], P(None, ('row', 'col')), may hold values from -6 to 6
- diagonal: float32 [4096], P(('row', 'col'))
- blocks: float32 [4, 8, 8, 128, 128], P('row', 'col'), may hold values from -0.125 to 0.125
- block_rows: int32 [4, 8, 8], P('row', 'col'), may hold values from 0 to 7
- block_cols: int32 [4, 8, 8], P('row', 'col'), may hold values from 0 to 3
- counts: int32 [4, 8], P('row', 'col'), may hold values from 4 to 8, as said below
Outputs:
- eigvecs: float32 [8, 4096], P(None, ('row', 'col'))
- factor: float32 [8, 8], replicated
The draws below stay inside these ranges and needn't reach their ends.
Inputs may be any that keep to these rules, and one draw needn't show every extreme that they name: `counts`: every device has at least half of its 8 slots live, and some device has all 8 live.
All inputs are finite; a program needn't handle non-finite values.
Results may differ from the reference program's by a relative error of at most 0.0001.
Values sent between devices are 32-bit elements; how exact they have to be, the bound alone decides.
No kernel may reach another device: no remote copies, remote signals or barrier semaphores. Data moves between devices by JAX's collectives and lax.ppermute only.
A program may use at most 64 MiB of HBM per device.

```python
import jax
import jax.numpy as jnp
from jax import lax

BS = 128
K = 8
ITERS = 4
BL = 8
NS = 4096
N_ROW = 4
N_COL = 8


def draw_diagonal(key, part):
    place = jnp.arange(NS).astype(jnp.float32) / NS
    rough = jnp.exp(jax.random.uniform(key, (NS,), jnp.float32, 0.0, jnp.log(3.0)))
    return rough * (1.0 + 2.0 * place)


def draw_counts(key, part):
    first = jax.random.fold_in(key, 11)
    second = jax.random.fold_in(key, 23)
    values = jax.random.randint(first, (N_ROW * N_COL,), BL // 2, BL + 1)
    spot = jax.random.randint(second, (), 0, N_ROW * N_COL)
    values = jnp.where(jnp.arange(N_ROW * N_COL) == spot, BL, values)
    return values.reshape(N_ROW, N_COL).astype(jnp.int32)


def plant(values, own_key, least, top_value):
    spot = [jax.random.randint(jax.random.fold_in(own_key, axis), (), 0, length) for axis, length in enumerate(values.shape)]
    main_axis = values.shape.index(max(values.shape))
    next_to = spot[:main_axis] + [(spot[main_axis] + 1) % values.shape[main_axis]] + spot[main_axis + 1:]
    return values.at[tuple(spot)].set(least).at[tuple(next_to)].set(top_value)


def block_levels(key, shape, split, low, top_value):
    gain = 1.0
    for position, parts in split:
        heights = jax.random.uniform(jax.random.fold_in(jax.random.fold_in(key, 6), position), (parts,), jnp.float32, low / len(split), top_value / len(split))
        gain = gain * jnp.repeat(jnp.exp(heights), shape[position] // parts).reshape((-1,) + (1,) * (len(shape) - 1 - position))
    return gain


def normal_values(rng, dims, width, bound, cuts=(), kind=jnp.bfloat16):
    entries = width * jax.random.normal(rng, dims, jnp.float32)
    if cuts:
        entries = entries * block_levels(rng, dims, cuts, -0.22, 0.18)
    return jnp.clip(entries, -bound, bound).astype(kind)


def setup_inputs(seed: int = 0) -> dict:
    seeds = jax.random.split(jax.random.key(seed), 7)
    return {
        "vectors": normal_values(seeds[0], (K, NS), 1.0, 6.0, ((1, 32),), jnp.float32),
        "diagonal": draw_diagonal(jax.random.fold_in(seeds[6], 71), 0),
        "blocks": normal_values(seeds[2], (N_ROW, N_COL, BL, BS, BS), (2 * BL * BS) ** -0.5, 0.125, ((0, 4), (1, 8)), jnp.float32),
        "block_rows": plant(jax.random.randint(seeds[3], (N_ROW, N_COL, BL), 0, N_COL), jax.random.fold_in(seeds[3], 1), 0, N_COL - 1).astype(jnp.int32),
        "block_cols": plant(jax.random.randint(seeds[4], (N_ROW, N_COL, BL), 0, N_ROW), jax.random.fold_in(seeds[4], 1), 0, N_ROW - 1).astype(jnp.int32),
        "counts": draw_counts(jax.random.fold_in(seeds[6], 71), 0),
    }


def reference(vectors, diagonal, blocks, block_rows, block_cols, counts):
    high = lax.Precision.HIGHEST
    nvec = vectors.shape[0]
    slots = jnp.arange(BL).astype(jnp.int32)
    live = (slots[None, None, :] < counts[:, :, None]).astype(jnp.float32)
    row_select = (block_rows[..., None] == jnp.arange(N_COL).astype(jnp.int32)).astype(jnp.float32) * live[..., None]
    col_select = (block_cols[..., None] == jnp.arange(N_ROW).astype(jnp.int32)).astype(jnp.float32) * live[..., None]
    blocks_f = blocks.astype(jnp.float32)
    current = vectors
    lower = jnp.eye(nvec, dtype=jnp.float32)
    for step in range(ITERS):
        grid_x = current.reshape(nvec, N_ROW, N_COL, BS)
        col_input = jnp.einsum('rcbq,kqcj->krcbj', col_select, grid_x, precision=high)
        direct = jnp.einsum('rcbij,krcbj->krcbi', blocks_f, col_input, precision=high)
        direct_sum = jnp.einsum('rcbq,krcbi->krqi', row_select, direct, precision=high).reshape(nvec, NS)
        row_input = jnp.einsum('rcbq,krqi->krcbi', row_select, grid_x, precision=high)
        transposed = jnp.einsum('rcbij,krcbi->krcbj', blocks_f, row_input, precision=high)
        transposed_sum = jnp.einsum('rcbq,krcbj->kqcj', col_select, transposed, precision=high).reshape(nvec, NS)
        images = diagonal[None, :] * current + direct_sum + transposed_sum
        gram = jnp.dot(images.astype(jnp.float32), images.T.astype(jnp.float32), precision=high, preferred_element_type=jnp.float32)
        lower = jnp.linalg.cholesky(gram)
        current = lax.linalg.triangular_solve(lower, images, left_side=True, lower=True)
    return (current, lower)
```

```python
import functools

import jax
import jax.numpy as jnp
from jax import lax
from jax.experimental import pallas as pl
from jax.experimental.pallas import tpu as pltpu
from jax.sharding import PartitionSpec as P

ITERS = 4
HIGH = lax.Precision.HIGHEST
NT = (((1,), (1,)), ((), ()))
NN = (((1,), (0,)), ((), ()))


def dot(a, b, dims):
    return lax.dot_general(a, b, dims, precision=HIGH, preferred_element_type=jnp.float32)


def factorize(gram, values):
    size = gram.shape[0]
    lanes = gram.shape[1]
    rows = lax.broadcasted_iota(jnp.int32, (size, 1), 0)
    row_grid = lax.broadcasted_iota(jnp.int32, (size, lanes), 0)
    lane_grid = lax.broadcasted_iota(jnp.int32, (size, lanes), 1)
    lower = jnp.zeros((size, lanes), jnp.float32)
    scale = jnp.zeros((size, 1), jnp.float32)
    values = list(values)
    for j in range(size):
        column = gram[:, j : j + 1]
        pivot = gram[j : j + 1, j : j + 1]
        root = 1.0 / jnp.sqrt(pivot)
        lower = jnp.where((lane_grid == j) & (row_grid >= j), column * root, lower)
        scale = jnp.where(rows == j, root, scale)
        factor = jnp.where(rows > j, column / pivot, 0.0)
        gram = gram - factor * gram[j : j + 1, :]
        values = [v - factor * v[j : j + 1, :] for v in values]
    return lower, [v * scale for v in values]


def images_of(own_ref, other_ref, slots, normalize):
    images = [own_ref[s] + other_ref[s] for s in range(slots)]
    if normalize:
        _, images = factorize(own_ref[slots] + other_ref[slots], images)
    return images


def direct_kernel(slots, normalize, meta_ref, own_ref, other_ref, tile_ref, send_ref, held_ref):
    nvec = send_ref.shape[1] // 2
    count = tile_ref.shape[0]
    for s, image in enumerate(images_of(own_ref, other_ref, slots, normalize)):
        held_ref[s] = image
    mine = held_ref[meta_ref[2 * count + 1]]
    parts = []
    for b in range(count):
        picked = held_ref[meta_ref[count + b]]
        picked = jnp.where(b < meta_ref[2 * count], picked, 0.0)
        parts.append(dot(picked, tile_ref[b], NT))
    for q in range(send_ref.shape[0]):
        send_ref[q, :nvec] = mine
        send_ref[q, nvec:] = jnp.zeros_like(mine)
    for b in range(count):
        send_ref[meta_ref[b], nvec:] += parts[b]


def transposed_kernel(slots, meta_ref, recv_ref, tile_ref, diag_ref, part_ref):
    cols, double, width = recv_ref.shape
    nvec = double // 2
    count = tile_ref.shape[0]
    parts = []
    for b in range(count):
        picked = recv_ref[meta_ref[b], :nvec]
        picked = jnp.where(b < meta_ref[2 * count], picked, 0.0)
        parts.append(dot(picked, tile_ref[b], NN))
    gram = None
    total = diag_ref[...] * recv_ref[meta_ref[2 * count + 2], :nvec]
    for c in range(cols):
        total = total + recv_ref[c, nvec:]
        piece = recv_ref[c, :nvec]
        term = dot(piece, piece, NT)
        gram = term if gram is None else gram + term
    part_ref[...] = jnp.zeros_like(part_ref)
    part_ref[slots, :, :nvec] = gram
    part_ref[meta_ref[2 * count + 1]] = total
    for b in range(count):
        part_ref[meta_ref[count + b]] += parts[b]


def last_images_kernel(slots, meta_ref, own_ref, other_ref, image_ref, send_ref, held_ref):
    nvec = send_ref.shape[1]
    gram = None
    for s, image in enumerate(images_of(own_ref, other_ref, slots, True)):
        held_ref[s] = image
        term = dot(image, image, NT)
        gram = term if gram is None else gram + term
    image_ref[...] = held_ref[meta_ref[meta_ref.shape[0] - 2]]
    gram = jnp.concatenate([gram, jnp.zeros((nvec, send_ref.shape[2] - nvec), jnp.float32)], axis=1)
    for q in range(send_ref.shape[0]):
        send_ref[q] = gram


def last_factor_kernel(image_ref, recv_ref, vector_ref, lower_ref):
    nvec = image_ref.shape[0]
    gram = recv_ref[0]
    for c in range(1, recv_ref.shape[0]):
        gram = gram + recv_ref[c]
    lower, values = factorize(gram, [image_ref[...]])
    vector_ref[...] = values[0]
    lower_ref[...] = lower[:, :nvec]


VMEM = pl.BlockSpec(memory_space=pltpu.VMEM)
SMEM = pl.BlockSpec(memory_space=pltpu.SMEM)


def shards(n_row, n_col, vectors, diagonal, blocks, block_rows, block_cols, counts):
    tile = blocks[0, 0]
    nvec, width = vectors.shape
    f32 = jnp.float32
    row, col = lax.axis_index("row"), lax.axis_index("col")
    meta = jnp.concatenate(
        [
            block_rows[0, 0],
            block_cols[0, 0],
            counts[0],
            jnp.stack([row, col]).astype(jnp.int32),
        ]
    )
    diag = diagonal[None, :]
    held = pltpu.VMEM((n_row, nvec, width), f32)
    pack = jax.ShapeDtypeStruct((n_row + 1, nvec, width), f32)
    wide = jax.ShapeDtypeStruct((n_col, 2 * nvec, width), f32)
    thin = jax.ShapeDtypeStruct((n_col, nvec, width), f32)
    piece = jax.ShapeDtypeStruct((nvec, width), f32)

    def exchange(value, step):
        return lax.ppermute(value, "row", [(i, i ^ step) for i in range(n_row)])

    def over_row(part):
        step = 1
        while 2 * step < n_row:
            part = part + exchange(part, step)
            step *= 2
        return part, exchange(part, step)

    slot = jnp.arange(n_row + 1)[:, None, None]
    part = jnp.where(slot == row, vectors[None], 0.0)
    for step in range(ITERS):
        own, other = over_row(part)
        send = pl.pallas_call(
            functools.partial(direct_kernel, n_row, step > 0),
            out_shape=wide,
            in_specs=[SMEM, VMEM, VMEM, VMEM],
            out_specs=VMEM,
            scratch_shapes=[held],
            name="direct",
        )(meta, own, other, tile)
        recv = lax.all_to_all(send, "col", 0, 0, tiled=True)
        part = pl.pallas_call(
            functools.partial(transposed_kernel, n_row),
            out_shape=pack,
            in_specs=[SMEM, VMEM, VMEM, VMEM],
            out_specs=VMEM,
            name="transposed",
        )(meta, recv, tile, diag)
    own, other = over_row(part)
    image, send = pl.pallas_call(
        functools.partial(last_images_kernel, n_row),
        out_shape=(piece, thin),
        in_specs=[SMEM, VMEM, VMEM],
        out_specs=(VMEM, VMEM),
        scratch_shapes=[held],
        name="last_images",
    )(meta, own, other)
    recv = lax.all_to_all(send, "col", 0, 0, tiled=True)
    return pl.pallas_call(
        last_factor_kernel,
        out_shape=(piece, jax.ShapeDtypeStruct((nvec, nvec), f32)),
        in_specs=[VMEM, VMEM],
        out_specs=(VMEM, VMEM),
        name="last_factor",
    )(image, recv)


def solution(mesh):
    n_row, n_col = mesh.shape["row"], mesh.shape["col"]
    if n_row & (n_row - 1) or n_row < 2:
        raise ValueError("uneven row")
    placed = (
        P(None, ("row", "col")),
        P(("row", "col")),
        P("row", "col", None, None, None),
        P("row", "col", None),
        P("row", "col", None),
        P("row", "col"),
    )
    return jax.shard_map(
        functools.partial(shards, n_row, n_col),
        mesh=mesh,
        in_specs=placed,
        out_specs=(P(None, ("row", "col")), P()),
        check_vma=False,
    )
```

```python
import functools

import jax
import jax.numpy as jnp
from jax import lax
from jax.experimental import pallas as pl
from jax.experimental.pallas import tpu as pltpu
from jax.sharding import PartitionSpec as P

ITERS = 4
HIGH = lax.Precision.HIGHEST
NT = (((1,), (1,)), ((), ()))
NN = (((1,), (0,)), ((), ()))


def dot(a, b, dims):
    return lax.dot_general(a, b, dims, precision=HIGH, preferred_element_type=jnp.float32)


def factorize(gram, values):
    size = gram.shape[0]
    lanes = gram.shape[1]
    rows = lax.broadcasted_iota(jnp.int32, (size, 1), 0)
    row_grid = lax.broadcasted_iota(jnp.int32, (size, lanes), 0)
    lane_grid = lax.broadcasted_iota(jnp.int32, (size, lanes), 1)
    lower = jnp.zeros((size, lanes), jnp.float32)
    scale = jnp.zeros((size, 1), jnp.float32)
    values = list(values)
    for j in range(size):
        column = gram[:, j : j + 1]
        pivot = gram[j : j + 1, j : j + 1]
        root = 1.0 / jnp.sqrt(pivot)
        lower = jnp.where((lane_grid == j) & (row_grid >= j), column * root, lower)
        scale = jnp.where(rows == j, root, scale)
        factor = jnp.where(rows > j, column / pivot, 0.0)
        gram = gram - factor * gram[j : j + 1, :]
        values = [v - factor * v[j : j + 1, :] for v in values]
    return lower, [v * scale for v in values]


def images_of(own_ref, other_ref, slots, normalize):
    images = [own_ref[s] + other_ref[s] for s in range(slots)]
    if normalize:
        _, images = factorize(own_ref[slots] + other_ref[slots], images)
    return images


def direct_kernel(slots, normalize, meta_ref, own_ref, other_ref, tile_ref, send_ref, held_ref):
    nvec = send_ref.shape[1] // 2
    count = tile_ref.shape[0]
    for s, image in enumerate(images_of(own_ref, other_ref, slots, normalize)):
        held_ref[s] = image
    mine = held_ref[meta_ref[2 * count + 1]]
    parts = []
    for b in range(count):
        picked = held_ref[meta_ref[count + b]]
        picked = jnp.where(b < meta_ref[2 * count], picked, 0.0)
        parts.append(dot(picked, tile_ref[b], NT))
    for q in range(send_ref.shape[0]):
        send_ref[q, :nvec] = mine
        send_ref[q, nvec:] = jnp.zeros_like(mine)
    for b in range(count):
        send_ref[meta_ref[b], nvec:] += parts[b]


def transposed_kernel(slots, meta_ref, recv_ref, tile_ref, diag_ref, part_ref):
    cols, double, width = recv_ref.shape
    nvec = double // 2
    count = tile_ref.shape[0]
    parts = []
    for b in range(count):
        picked = recv_ref[meta_ref[b], :nvec]
        picked = jnp.where(b < meta_ref[2 * count], picked, 0.0)
        parts.append(dot(picked, tile_ref[b], NN))
    gram = None
    total = diag_ref[...] * recv_ref[meta_ref[2 * count + 2], :nvec]
    for c in range(cols):
        total = total + recv_ref[c, nvec:]
        piece = recv_ref[c, :nvec]
        term = dot(piece, piece, NT)
        gram = term if gram is None else gram + term
    part_ref[...] = jnp.zeros_like(part_ref)
    part_ref[slots, :, :nvec] = gram
    part_ref[meta_ref[2 * count + 1]] = total
    for b in range(count):
        part_ref[meta_ref[count + b]] += parts[b]


def last_images_kernel(slots, meta_ref, own_ref, other_ref, image_ref, send_ref, held_ref):
    nvec = send_ref.shape[1]
    gram = None
    for s, image in enumerate(images_of(own_ref, other_ref, slots, True)):
        held_ref[s] = image
        term = dot(image, image, NT)
        gram = term if gram is None else gram + term
    image_ref[...] = held_ref[meta_ref[meta_ref.shape[0] - 2]]
    gram = jnp.concatenate([gram, jnp.zeros((nvec, send_ref.shape[2] - nvec), jnp.float32)], axis=1)
    for q in range(send_ref.shape[0]):
        send_ref[q] = gram


def last_factor_kernel(image_ref, recv_ref, vector_ref, lower_ref):
    nvec = image_ref.shape[0]
    gram = recv_ref[0]
    for c in range(1, recv_ref.shape[0]):
        gram = gram + recv_ref[c]
    lower, values = factorize(gram, [image_ref[...]])
    vector_ref[...] = values[0]
    lower_ref[...] = lower[:, :nvec]


VMEM = pl.BlockSpec(memory_space=pltpu.VMEM)
SMEM = pl.BlockSpec(memory_space=pltpu.SMEM)


def call(kernel, name, outs, meta, *operands, scratch=()):
    specs = [VMEM] * len(operands)
    operands = [pltpu.with_memory_space_constraint(x, pltpu.VMEM) for x in operands]
    if meta is not None:
        specs = [SMEM, *specs]
        operands = [pltpu.with_memory_space_constraint(meta, pltpu.SMEM), *operands]
    return pl.pallas_call(
        kernel,
        out_shape=outs,
        in_specs=specs,
        out_specs=jax.tree.map(lambda _: VMEM, outs),
        scratch_shapes=scratch,
        name=name,
    )(*operands)


def shards(n_row, n_col, vectors, diagonal, blocks, block_rows, block_cols, counts):
    tile = blocks[0, 0]
    nvec, width = vectors.shape
    f32 = jnp.float32
    row, col = lax.axis_index("row"), lax.axis_index("col")
    meta = jnp.concatenate(
        [
            block_rows[0, 0],
            block_cols[0, 0],
            counts[0],
            jnp.stack([row, col]).astype(jnp.int32),
        ]
    )
    diag = diagonal[None, :]
    held = pltpu.VMEM((n_row, nvec, width), f32)
    pack = pltpu.VMEM((n_row + 1, nvec, width), f32)
    wide = pltpu.VMEM((n_col, 2 * nvec, width), f32)
    thin = pltpu.VMEM((n_col, nvec, width), f32)
    piece = pltpu.VMEM((nvec, width), f32)

    def exchange(value, step):
        return lax.ppermute(value, "row", [(i, i ^ step) for i in range(n_row)])

    def over_row(part):
        step = 1
        while 2 * step < n_row:
            part = part + exchange(part, step)
            step *= 2
        return part, exchange(part, step)

    slot = jnp.arange(n_row + 1)[:, None, None]
    part = jnp.where(slot == row, vectors[None], 0.0)
    for step in range(ITERS):
        own, other = over_row(part)
        kernel = functools.partial(direct_kernel, n_row, step > 0)
        send = call(kernel, "direct", wide, meta, own, other, tile, scratch=[held])
        recv = lax.all_to_all(send, "col", 0, 0, tiled=True)
        kernel = functools.partial(transposed_kernel, n_row)
        part = call(kernel, "transposed", pack, meta, recv, tile, diag)
    own, other = over_row(part)
    kernel = functools.partial(last_images_kernel, n_row)
    image, send = call(kernel, "last_images", (piece, thin), meta, own, other, scratch=[held])
    recv = lax.all_to_all(send, "col", 0, 0, tiled=True)
    outs = (
        jax.ShapeDtypeStruct((nvec, width), f32),
        jax.ShapeDtypeStruct((nvec, nvec), f32),
    )
    return call(last_factor_kernel, "last_factor", outs, None, image, recv)


def solution(mesh):
    n_row, n_col = mesh.shape["row"], mesh.shape["col"]
    if n_row & (n_row - 1) or n_row < 2:
        raise ValueError("uneven row")
    placed = (
        P(None, ("row", "col")),
        P(("row", "col")),
        P("row", "col", None, None, None),
        P("row", "col", None),
        P("row", "col", None),
        P("row", "col"),
    )
    return jax.shard_map(
        functools.partial(shards, n_row, n_col),
        mesh=mesh,
        in_specs=placed,
        out_specs=(P(None, ("row", "col")), P()),
        check_vma=False,
    )
```
